32 devices in a mesh: group: 2 (over y), expert: 4 (over z), etp: 4 (over x, core).
Axes of the slice: x: 2, y: 2, z: 4, core: 2. Of those that a mesh axis runs over, the one named last changes fastest.
Arguments:
- tokens: bfloat16 [128, 4096], P(('group', 'expert')), parts along dimension 0, may hold values from -6 to 6
- expert_ids: int32 [128, 2], P(('group', 'expert')), parts along dimension 0, may hold values from 0 to 3, all different within a row; in each aligned block of 4 rows (0 to 3, 4 to 7, ...) at most 4 rows name the same one
- route_weights: float32 [128, 2], P(('group', 'expert', 'etp')), parts along dimension 0, may hold values from 0.05 to 1
- w_gate: bfloat16 [4, 1536, 4096], P('expert', 'etp'), may hold values from -0.09375 to 0.09375
- w_up: bfloat16 [4, 1536, 4096], P('expert', 'etp'), may hold values from -0.09375 to 0.09375
- w_down: bfloat16 [4, 1536, 4096], P('expert', 'etp'), may hold values from -0.15625 to 0.15625
Outputs:
- mixed: bfloat16 [128, 4096], P(('group', 'expert', 'etp')), parts along dimension 0
The draws below stay inside these ranges and needn't reach their ends.
There are 2 independent parts, one for each index of `group`. The reference program is written for one: setup_inputs(seed, part) draws one part's arguments, and reference() takes and returns one part's arrays. A program takes and returns all parts, laid end to end along the dimension named above; an argument that names none is the same for every part. Nothing has to cross between parts.
Inputs may be any that keep to these rules, and one draw needn't show every extreme that they name: `expert_ids`: each row names 2 different experts; in each aligned block of 4 rows no expert is named by more than 4 rows, a bound that some block reaches.
All inputs are finite; a program needn't handle non-finite values.
Results may differ from the reference program's by a relative error of at most 0.015.
Values may be sent and summed in bfloat16 or wider, within the bound.
A program may use at most 64 MiB of HBM per device.

```python
import math
import jax
import jax.numpy as jnp
import numpy as np
from jax import lax

D = 4096
FF = 1536
ROWS_DEV = 4
EXPERTS = 4
TOP = 2
CAPSUB = 4
TOKENS = 64
NBLK = 16
N_ETP = 4


def block_scale(rng, extent, shards, smallest, largest):
    loudness = 1.0
    for position, shards_of in shards:
        steps = jax.random.uniform(jax.random.fold_in(jax.random.fold_in(rng, 6), position), (shards_of,), jnp.float32, smallest / len(shards), largest / len(shards))
        loudness = loudness * jnp.repeat(jnp.exp(steps), extent[position] // shards_of).reshape((-1,) + (1,) * (len(extent) - 1 - position))
    return loudness


def deal_out(key, own, number, rows, number_of, top, reach, slope):
    order = jax.random.permutation(key, number_of)
    crowded, common = shares(number_of, rows * top, reach, slope, True), shares(number_of, rows * top, reach, slope, False)
    places = jnp.arange(number_of)

    def named(tallies, offset_by):
        used = int((tallies > 0).sum())
        fixed = max(1, used // 4)
        moved = fixed + (places - fixed + offset_by * (used - fixed)) % max(1, number_of - fixed)
        return jnp.zeros((number_of,), jnp.int32).at[order[jnp.where(places < fixed, places, moved)]].set(jnp.asarray(tallies, jnp.int32))

    tallies = jnp.where(number % 4 == 0, named(crowded, number // 4), named(common, number - number // 4 - 1))
    mixed = jax.random.permutation(jax.random.fold_in(own, 3), number_of)
    donor, taker = mixed[0:number_of // 2 * 2:2], mixed[1:number_of // 2 * 2:2]
    room = jnp.minimum(tallies[donor] - 1, reach - tallies[taker]) // 2
    room = jnp.where((donor == order[0]) | (taker == order[0]) | (tallies[taker] == 0), 0, jnp.maximum(room, 0))
    moved = jax.random.randint(jax.random.fold_in(own, 4), (number_of // 2,), 0, 1 << 20) % (room + 1)
    tallies = tallies.at[donor].add(-moved).at[taker].add(moved)
    members = jnp.searchsorted(jnp.cumsum(tallies), jnp.arange(rows * top), side="right").astype(jnp.int32)
    listing = members.reshape(top, rows).T
    listing = listing[jax.random.permutation(jax.random.fold_in(own, 1), rows)]
    offset_by = jax.random.randint(jax.random.fold_in(own, 2), (rows, 1), 0, top)
    return jnp.take_along_axis(listing, (jnp.arange(top)[None, :] + offset_by) % top, axis=1)


def shares(number_of, total, reach, slope, full):
    weights = [(1 << 20) // math.isqrt(rank ** slope) + 1 for rank in range(1, number_of + 1)]
    largest = reach if full else min(reach, max(-(-total // number_of), total * weights[0] // sum(weights)))
    least = 1 if total - largest >= number_of - 1 else 0
    counts, spare = [largest] + [least] * (number_of - 1), total - largest - least * (number_of - 1)
    while spare > 0:
        free = [i for i in range(1, number_of) if counts[i] < largest] or [i for i in range(1, number_of) if counts[i] < reach]
        whole, left = sum([weights[i] for i in free]), spare
        for i in free:
            extra = min(reach - counts[i], max(1, left * weights[i] // whole), spare)
            counts[i] = counts[i] + extra
            spare = spare - extra
    return np.array(counts)


def normal_values(stream_key, extent, width, bound, cuts=(), held_as=jnp.bfloat16):
    gain = block_scale(stream_key, extent, cuts, -0.22, 0.18) if cuts else 1.0
    array = jax.random.normal(stream_key, extent, jnp.float32) * width * gain
    return jnp.minimum(jnp.maximum(array, -bound), bound).astype(held_as)


def setup_inputs(seed: int = 0, part: int = 0) -> dict:
    key_list = jax.random.split(jax.random.key(seed), 7)
    part_keys = jax.random.split(jax.random.fold_in(key_list[6], part), 7)
    tokens = normal_values(part_keys[0], (TOKENS, D), 1.0, 6.0, ((0, 4),))
    expert_ids_keys = jax.random.split(jax.random.fold_in(part_keys[1], 1), TOKENS // ROWS_DEV)
    expert_ids_turns = jax.random.permutation(jax.random.fold_in(part_keys[1], 3), TOKENS // ROWS_DEV)
    expert_ids = jax.vmap(lambda own, number: deal_out(jax.random.fold_in(part_keys[1], 2), own, number, ROWS_DEV, EXPERTS, TOP, CAPSUB, 2))(expert_ids_keys, expert_ids_turns).reshape((TOKENS, TOP))
    route_weights = jnp.clip(jnp.exp(math.log(1.0) - 2.9957323 * jax.random.uniform(part_keys[2], (TOKENS, TOP), jnp.float32) ** block_scale(part_keys[2], (TOKENS, TOP), ((0, 16),), -0.2, 0.2)), 0.05, 1.0)
    w_gate = normal_values(key_list[3], (EXPERTS, FF, D), D ** -0.5, 0.09375, ((0, 4), (1, 4)))
    w_up = normal_values(key_list[4], (EXPERTS, FF, D), D ** -0.5, 0.09375, ((0, 4), (1, 4)))
    w_down = normal_values(key_list[5], (EXPERTS, FF, D), FF ** -0.5, 0.15625, ((0, 4), (1, 4)))
    return dict(tokens=tokens, expert_ids=expert_ids, route_weights=route_weights, w_gate=w_gate, w_up=w_up, w_down=w_down)


def reference(tokens, expert_ids, route_weights, w_gate, w_up, w_down):
    ffd = FF // N_ETP
    flat = expert_ids.reshape(-1)
    count = flat.shape[0]
    row = jnp.arange(count, dtype=jnp.int32) // TOP
    block = row // ROWS_DEV
    by_block = expert_ids.reshape(NBLK, ROWS_DEV * TOP)
    onehot = (by_block[:, :, None] == jnp.arange(EXPERTS, dtype=jnp.int32)[None, None, :]).astype(jnp.int32)
    ranks = jnp.cumsum(onehot, axis=1) - onehot
    slot = jnp.sum(ranks * onehot, axis=2).reshape(-1)
    pos = (flat * (NBLK * CAPSUB) + block * CAPSUB + slot).astype(jnp.int32)
    source = jnp.zeros((EXPERTS * NBLK * CAPSUB,), jnp.int32).at[pos].set(row)

    def one_expert(items):
        index, gate_e, up_e, down_e = items
        rows_in = tokens[index]
        gate = jnp.dot(rows_in, gate_e.T, preferred_element_type=jnp.float32)
        upper = jnp.dot(rows_in, up_e.T, preferred_element_type=jnp.float32)
        hidden = (jax.nn.silu(gate) * upper).astype(jnp.bfloat16)
        parts = jnp.einsum('rsf,sfd->rsd', hidden.reshape(-1, N_ETP, ffd).astype(jnp.float32),
                           down_e.reshape(N_ETP, ffd, D).astype(jnp.float32))
        parts = lax.optimization_barrier(parts.astype(jnp.bfloat16)).astype(jnp.float32)
        return jnp.sum(parts, axis=1).astype(jnp.bfloat16)

    results = lax.map(one_expert, (source.reshape(EXPERTS, NBLK * CAPSUB), w_gate, w_up, w_down))
    picked = results.reshape(-1, D)[pos].astype(jnp.float32).reshape(TOKENS, TOP, D)
    combine = route_weights / jnp.sum(route_weights, axis=1, keepdims=True)
    return jnp.sum(picked * combine[:, :, None], axis=1).astype(jnp.bfloat16)
```

```python
import functools

import jax
import jax.numpy as jnp
from jax import lax
from jax.experimental import pallas as pl
from jax.experimental.pallas import tpu as pltpu
from jax.sharding import PartitionSpec as P

MESH = pl.DeviceIdType.MESH
BF16 = jnp.bfloat16
F32 = jnp.float32


def layer_kernel(
    n_exp, n_etp, n_chunk,
    tok_ref, ids_ref, rw_ref, wg_ref, wu_ref, wd_ref, out_ref,
    xbuf, wgb, wub, wdb, pbuf, recva, sendb, recvb, ownb, sendc, recvc,
    wsem, dsem, tsem, zs, zr, xs, xr, cs, cr, as_, ar, bs, br, es, er,
):
    n_x = n_etp // 2
    rows = tok_ref.shape[0]
    own_rows = rows // n_etp
    width = tok_ref.shape[1]
    kq = width // n_etp
    cw = width // n_chunk
    grp = n_exp * own_rows
    e = lax.axis_index("expert")
    q = lax.axis_index("etp")
    x = q // 2
    c = q % 2

    def etp_of(co, xo):
        return lax.rem(x + xo, n_x) * 2 + lax.rem(c + co, 2)

    slots = [(co, xo) for xo in range(n_x) for co in range(2)]

    def quarter(co, xo):
        return pl.ds(pl.multiple_of(etp_of(co, xo) * kq, kq), kq)

    tok_copies, w_copies, d_copies = {}, {}, []
    for co, xo in slots:
        i = co * n_x + xo
        t = pltpu.make_async_copy(tok_ref.at[:, quarter(co, xo)], xbuf.at[i, e], tsem.at[i])
        t.start()
        tok_copies[i] = t
    for co, xo in slots:
        i = co * n_x + xo
        a = pltpu.make_async_copy(wg_ref.at[0, :, quarter(co, xo)], wgb.at[i], wsem.at[i, 0])
        b = pltpu.make_async_copy(wu_ref.at[0, :, quarter(co, xo)], wub.at[i], wsem.at[i, 1])
        a.start()
        b.start()
        w_copies[i] = (a, b)
    for j in range(n_chunk):
        d = pltpu.make_async_copy(wd_ref.at[0, :, pl.ds(j * cw, cw)], wdb.at[j], dsem.at[j])
        d.start()
        d_copies.append(d)

    barrier = pltpu.get_barrier_semaphore()
    partners = [{"etp": etp_of(1, 0)}]
    partners += [{"etp": etp_of(0, xo)} for xo in range(1, n_x)]
    partners += [{"expert": lax.rem(e + k, n_exp)} for k in range(1, n_exp)]
    for dev in partners:
        pl.semaphore_signal(barrier, inc=1, device_id=dev, device_id_type=MESH)
    pl.semaphore_wait(barrier, len(partners))

    pending = []
    z_copies = []
    for k in range(1, n_exp):
        cp = pltpu.make_async_remote_copy(
            tok_ref.at[:, quarter(0, 0)], xbuf.at[0, e], zs.at[k - 1], zr.at[k - 1],
            device_id={"expert": lax.rem(e + k, n_exp)}, device_id_type=MESH)
        cp.start()
        z_copies.append(cp)
        pending.append(cp)

    x_copies, c_copies = {}, {}

    def to_core(xo, k):
        blk = lax.rem(e + n_exp - k, n_exp)
        cp = pltpu.make_async_remote_copy(
            xbuf.at[xo, blk], xbuf.at[n_x + xo, blk], cs.at[xo, k - 1], cr.at[xo, k - 1],
            device_id={"etp": etp_of(1, 0)}, device_id_type=MESH)
        cp.start()
        c_copies[xo, k] = cp
        pending.append(cp)

    for k in range(1, n_exp):
        blk = lax.rem(e + n_exp - k, n_exp)
        z_copies[k - 1].wait_recv()
        for xo in range(1, n_x):
            cp = pltpu.make_async_remote_copy(
                xbuf.at[0, blk], xbuf.at[n_x - xo, blk], xs.at[xo - 1, k - 1], xr.at[xo - 1, k - 1],
                device_id={"etp": etp_of(0, xo)}, device_id_type=MESH)
            cp.start()
            x_copies[xo, k] = cp
            pending.append(cp)
        to_core(0, k)

    def partial_dots(i):
        tok_copies[i].wait()
        w_copies[i][0].wait()
        w_copies[i][1].wait()
        xv = xbuf[i].reshape(n_exp * rows, kq)
        dims = (((1,), (1,)), ((), ()))
        return (lax.dot_general(xv, wgb[i], dims, preferred_element_type=F32),
                lax.dot_general(xv, wub[i], dims, preferred_element_type=F32))

    gate, upper = partial_dots(0)
    for xo in range(1, n_x):
        for k in range(1, n_exp):
            x_copies[xo, k].wait_recv()
            to_core(n_x - xo, k)
    for co, xo in slots[1:]:
        if co == 1:
            for k in range(1, n_exp):
                c_copies[xo, k].wait_recv()
        g, u = partial_dots(co * n_x + xo)
        gate += g
        upper += u
    hidden = (gate / (1.0 + jnp.exp(-gate)) * upper).astype(BF16)

    total = n_exp * rows
    m = lax.broadcasted_iota(jnp.int32, (total, total), 0)
    n = lax.broadcasted_iota(jnp.int32, (total, total), 1)
    slot = m // grp
    dest = lax.rem(x + slot % n_x, n_x) * 2 + lax.rem(c + slot // n_x, 2)
    source = (m % grp) // own_rows * rows + dest * own_rows + m % own_rows
    perm = (n == source).astype(F32).astype(BF16)
    hidden = jnp.dot(perm, hidden, preferred_element_type=F32).astype(BF16)

    half = n_x * grp
    a_copies, b_copies, e_copies = [], {}, {}
    for j in range(n_chunk):
        d_copies[j].wait()
        pbuf[j] = jnp.dot(hidden, wdb[j], preferred_element_type=F32).astype(BF16)
        cp = pltpu.make_async_remote_copy(
            pbuf.at[j, pl.ds(half, half)], recva.at[j], as_.at[j], ar.at[j],
            device_id={"etp": etp_of(1, 0)}, device_id_type=MESH)
        cp.start()
        a_copies.append(cp)
        pending.append(cp)

    for j in range(n_chunk):
        a_copies[j].wait_recv()
        for xo in range(1, n_x):
            at = pl.ds(xo * grp, grp)
            sendb[j, xo - 1] = (pbuf[j, at].astype(F32) + recva[j, at].astype(F32)).astype(BF16)
            cp = pltpu.make_async_remote_copy(
                sendb.at[j, xo - 1], recvb.at[j, xo - 1], bs.at[j, xo - 1], br.at[j, xo - 1],
                device_id={"etp": etp_of(0, xo)}, device_id_type=MESH)
            cp.start()
            b_copies[j, xo] = cp
            pending.append(cp)
        at = pl.ds(0, grp)
        ownb[j] = pbuf[j, at].astype(F32) + recva[j, at].astype(F32)

    for j in range(n_chunk):
        total_j = ownb[j]
        for xo in range(1, n_x):
            b_copies[j, xo].wait_recv()
            total_j += recvb[j, xo - 1].astype(F32)
        total_j = total_j.astype(BF16)
        for z in range(n_exp):
            sendc[j, z] = total_j[z * own_rows:(z + 1) * own_rows]
        for k in range(1, n_exp):
            to = lax.rem(e + k, n_exp)
            cp = pltpu.make_async_remote_copy(
                sendc.at[j, to], recvc.at[j, k], es.at[j, k - 1], er.at[j, k - 1],
                device_id={"expert": to}, device_id_type=MESH)
            cp.start()
            e_copies[j, k] = cp
            pending.append(cp)

    ids = ids_ref[pl.ds(0, own_rows), :]
    for t in range(1, n_etp):
        ids = jnp.where(q == t, ids_ref[pl.ds(t * own_rows, own_rows), :], ids)
    rw = rw_ref[...]
    combine = rw / jnp.sum(rw, axis=1, keepdims=True)
    weights = []
    for k in range(n_exp):
        src = lax.rem(e + n_exp - k, n_exp)
        weights.append(jnp.sum(jnp.where(ids == src, combine, 0.0), axis=1, keepdims=True))

    for j in range(n_chunk):
        mixed = sendc[j, e].astype(F32) * weights[0]
        for k in range(1, n_exp):
            e_copies[j, k].wait_recv()
            mixed += recvc[j, k].astype(F32) * weights[k]
        out_ref[:, pl.ds(j * cw, cw)] = mixed.astype(BF16)

    for cp in pending:
        cp.wait_send()


def on_device(tokens, expert_ids, route_weights, w_gate, w_up, w_down):
    n_exp = lax.axis_size("expert")
    n_etp = lax.axis_size("etp")
    rows, width = tokens.shape
    own_rows = rows // n_etp
    exp_dev, ff, _ = w_gate.shape
    assert exp_dev == 1 and n_etp % 2 == 0
    n_x = n_etp // 2
    n_chunk = 4
    kq, cw, grp = width // n_etp, width // n_chunk, n_exp * own_rows
    half = n_x * grp
    dma = pltpu.SemaphoreType.DMA
    vmem = pl.BlockSpec(memory_space=pltpu.VMEM)
    hbm = pl.BlockSpec(memory_space=pl.ANY)
    return pl.pallas_call(
        functools.partial(layer_kernel, n_exp, n_etp, n_chunk),
        out_shape=jax.ShapeDtypeStruct((own_rows, width), BF16),
        in_specs=[hbm, vmem, vmem, hbm, hbm, hbm],
        out_specs=vmem,
        scratch_shapes=[
            pltpu.VMEM((n_etp, n_exp, rows, kq), BF16),
            pltpu.VMEM((n_etp, ff, kq), BF16),
            pltpu.VMEM((n_etp, ff, kq), BF16),
            pltpu.VMEM((n_chunk, ff, cw), BF16),
            pltpu.VMEM((n_chunk, 2 * half, cw), BF16),
            pltpu.VMEM((n_chunk, half, cw), BF16),
            pltpu.VMEM((n_chunk, n_x - 1, grp, cw), BF16),
            pltpu.VMEM((n_chunk, n_x - 1, grp, cw), BF16),
            pltpu.VMEM((n_chunk, grp, cw), F32),
            pltpu.VMEM((n_chunk, n_exp, own_rows, cw), BF16),
            pltpu.VMEM((n_chunk, n_exp, own_rows, cw), BF16),
            dma((n_etp, 2)),
            dma((n_chunk,)),
            dma((n_etp,)),
            dma((n_exp - 1,)), dma((n_exp - 1,)),
            dma((n_x - 1, n_exp - 1)), dma((n_x - 1, n_exp - 1)),
            dma((n_x, n_exp - 1)), dma((n_x, n_exp - 1)),
            dma((n_chunk,)), dma((n_chunk,)),
            dma((n_chunk, n_x - 1)), dma((n_chunk, n_x - 1)),
            dma((n_chunk, n_exp - 1)), dma((n_chunk, n_exp - 1)),
        ],
        compiler_params=pltpu.CompilerParams(collective_id=0, has_side_effects=True),
    )(tokens, expert_ids, route_weights, w_gate, w_up, w_down)


def solution(mesh):
    in_specs = (
        P(("group", "expert"), None),
        P(("group", "expert"), None),
        P(("group", "expert", "etp"), None),
        P("expert", "etp", None),
        P("expert", "etp", None),
        P("expert", "etp", None),
    )
    out_specs = P(("group", "expert", "etp"), None)
    return jax.shard_map(
        on_device, mesh=mesh, in_specs=in_specs, out_specs=out_specs, check_vma=False
    )
```

```python
import functools

import jax
import jax.numpy as jnp
from jax import lax
from jax.experimental import pallas as pl
from jax.experimental.pallas import tpu as pltpu
from jax.sharding import PartitionSpec as P

MESH = pl.DeviceIdType.MESH
BF16 = jnp.bfloat16
F32 = jnp.float32


def layer_kernel(
    n_exp, n_etp, n_chunk,
    tok_ref, ids_ref, rw_ref, wg_ref, wu_ref, wd_ref, out_ref,
    xbuf, wgb, wub, wdb, pbuf, recva, sendb, recvb, ownb, sendc, recvc,
    idsb, rwb, ssem, wsem, dsem, tsem, zs, zr, xs, xr, cs, cr, as_, ar, bs, br, es, er,
):
    n_x = n_etp // 2
    rows = tok_ref.shape[0]
    own_rows = rows // n_etp
    width = tok_ref.shape[1]
    kq = width // n_etp
    cw = width // n_chunk
    grp = n_exp * own_rows
    e = lax.axis_index("expert")
    q = lax.axis_index("etp")
    x = q // 2
    c = q % 2

    def etp_of(co, xo):
        return lax.rem(x + xo, n_x) * 2 + lax.rem(c + co, 2)

    high = e // (n_exp // 2)

    def farthest(k):
        down, up = n_exp - 1 - k, k
        down = down - (e - down + n_exp) // n_exp
        up = up + (up - e + n_exp) // n_exp
        return (1 - high) * down + high * up

    far = [farthest(k) for k in range(n_exp - 1)]
    near = far[::-1]

    slots = [(co, xo) for xo in range(n_x) for co in range(2)]

    def quarter(co, xo):
        return pl.ds(pl.multiple_of(etp_of(co, xo) * kq, kq), kq)

    tok_copies, w_copies, d_copies = {}, {}, []
    for co, xo in slots:
        i = co * n_x + xo
        t = pltpu.make_async_copy(tok_ref.at[:, quarter(co, xo)], xbuf.at[i, e], tsem.at[i])
        t.start()
        tok_copies[i] = t
    for co, xo in slots:
        i = co * n_x + xo
        a = pltpu.make_async_copy(wg_ref.at[0, :, quarter(co, xo)], wgb.at[i], wsem.at[i, 0])
        b = pltpu.make_async_copy(wu_ref.at[0, :, quarter(co, xo)], wub.at[i], wsem.at[i, 1])
        a.start()
        b.start()
        w_copies[i] = (a, b)
    for j in range(n_chunk):
        d = pltpu.make_async_copy(wd_ref.at[0, :, pl.ds(j * cw, cw)], wdb.at[j], dsem.at[j])
        d.start()
        d_copies.append(d)

    small_copies = [pltpu.make_async_copy(ids_ref, idsb, ssem.at[0]),
                    pltpu.make_async_copy(rw_ref, rwb, ssem.at[1])]
    for cp in small_copies:
        cp.start()
    barrier = pltpu.get_barrier_semaphore()
    partners = [{"etp": etp_of(1, 0)}]
    partners += [{"etp": etp_of(0, xo)} for xo in range(1, n_x)]
    partners += [{"expert": lax.rem(e + k, n_exp)} for k in range(1, n_exp)]
    for dev in partners:
        pl.semaphore_signal(barrier, inc=1, device_id=dev, device_id_type=MESH)
    pl.semaphore_wait(barrier, len(partners))

    pending = []
    for to in far:
        cp = pltpu.make_async_remote_copy(
            tok_ref.at[:, quarter(0, 0)], xbuf.at[0, e], zs.at[to], zr.at[e],
            device_id={"expert": to}, device_id_type=MESH)
        cp.start()
        pending.append(cp)

    def z_arrival(src):
        return pltpu.make_async_remote_copy(
            tok_ref.at[:, quarter(0, 0)], xbuf.at[0, src], zs.at[src], zr.at[src],
            device_id={"expert": src}, device_id_type=MESH)

    x_copies, c_copies = {}, {}

    def to_core(xo, k):
        blk = near[k - 1]
        cp = pltpu.make_async_remote_copy(
            xbuf.at[xo, blk], xbuf.at[n_x + xo, blk], cs.at[xo, k - 1], cr.at[xo, k - 1],
            device_id={"etp": etp_of(1, 0)}, device_id_type=MESH)
        cp.start()
        c_copies[xo, k] = cp
        pending.append(cp)

    for k in range(1, n_exp):
        blk = near[k - 1]
        z_arrival(blk).wait_recv()
        for xo in range(1, n_x):
            cp = pltpu.make_async_remote_copy(
                xbuf.at[0, blk], xbuf.at[n_x - xo, blk], xs.at[xo - 1, k - 1], xr.at[xo - 1, k - 1],
                device_id={"etp": etp_of(0, xo)}, device_id_type=MESH)
            cp.start()
            x_copies[xo, k] = cp
            pending.append(cp)
        to_core(0, k)

    def partial_dots(i):
        tok_copies[i].wait()
        w_copies[i][0].wait()
        w_copies[i][1].wait()
        xv = xbuf[i].reshape(n_exp * rows, kq)
        dims = (((1,), (1,)), ((), ()))
        return (lax.dot_general(xv, wgb[i], dims, preferred_element_type=F32),
                lax.dot_general(xv, wub[i], dims, preferred_element_type=F32))

    gate, upper = partial_dots(0)
    for xo in range(1, n_x):
        for k in range(1, n_exp):
            x_copies[xo, k].wait_recv()
            to_core(n_x - xo, k)
    for co, xo in slots[1:]:
        if co == 1:
            for k in range(1, n_exp):
                c_copies[xo, k].wait_recv()
        g, u = partial_dots(co * n_x + xo)
        gate += g
        upper += u
    hidden = (gate / (1.0 + jnp.exp(-gate)) * upper).astype(BF16)

    total = n_exp * rows
    m = lax.broadcasted_iota(jnp.int32, (total, total), 0)
    n = lax.broadcasted_iota(jnp.int32, (total, total), 1)
    slot = m // grp
    dest = lax.rem(x + slot % n_x, n_x) * 2 + lax.rem(c + slot // n_x, 2)
    source = (m % grp) // own_rows * rows + dest * own_rows + m % own_rows
    perm = (n == source).astype(F32).astype(BF16)
    hidden = jnp.dot(perm, hidden, preferred_element_type=F32).astype(BF16)

    half = n_x * grp
    a_copies, b_copies = [], {}
    for j in range(n_chunk):
        d_copies[j].wait()
        pbuf[j] = jnp.dot(hidden, wdb[j], preferred_element_type=F32).astype(BF16)
        cp = pltpu.make_async_remote_copy(
            pbuf.at[j, pl.ds(half, half)], recva.at[j], as_.at[j], ar.at[j],
            device_id={"etp": etp_of(1, 0)}, device_id_type=MESH)
        cp.start()
        a_copies.append(cp)
        pending.append(cp)

    for j in range(n_chunk):
        a_copies[j].wait_recv()
        for xo in range(1, n_x):
            at = pl.ds(xo * grp, grp)
            sendb[j, xo - 1] = (pbuf[j, at].astype(F32) + recva[j, at].astype(F32)).astype(BF16)
            cp = pltpu.make_async_remote_copy(
                sendb.at[j, xo - 1], recvb.at[j, xo - 1], bs.at[j, xo - 1], br.at[j, xo - 1],
                device_id={"etp": etp_of(0, xo)}, device_id_type=MESH)
            cp.start()
            b_copies[j, xo] = cp
            pending.append(cp)
        at = pl.ds(0, grp)
        ownb[j] = pbuf[j, at].astype(F32) + recva[j, at].astype(F32)

    for j in range(n_chunk):
        total_j = ownb[j]
        for xo in range(1, n_x):
            b_copies[j, xo].wait_recv()
            total_j += recvb[j, xo - 1].astype(F32)
        total_j = total_j.astype(BF16)
        for z in range(n_exp):
            sendc[j, z] = total_j[z * own_rows:(z + 1) * own_rows]
        for to in far:
            cp = pltpu.make_async_remote_copy(
                sendc.at[j, to], recvc.at[j, e], es.at[j, to], er.at[j, e],
                device_id={"expert": to}, device_id_type=MESH)
            cp.start()
            pending.append(cp)

    for cp in small_copies:
        cp.wait()
    top = idsb.shape[0]

    def column(row, first):
        lanes = lax.broadcasted_iota(jnp.int32, (own_rows, row.shape[1]), 1)
        here = lax.broadcasted_iota(jnp.int32, (own_rows, row.shape[1]), 0) + first
        return jnp.sum(jnp.where(lanes == here, row, jnp.zeros_like(row)), axis=1, keepdims=True)

    rws = rwb[...]
    combine = rws / jnp.sum(rws, axis=0, keepdims=True)
    chosen = [column(idsb[k:k + 1, :], q * own_rows) for k in range(top)]
    share = [column(combine[k:k + 1, :], 0) for k in range(top)]
    weights = []
    for src in [e] + near:
        weights.append(sum(jnp.where(i == src, w, 0.0) for i, w in zip(chosen, share)))

    for j in range(n_chunk):
        mixed = sendc[j, e].astype(F32) * weights[0]
        for k, src in enumerate(near):
            pltpu.make_async_remote_copy(
                sendc.at[j, src], recvc.at[j, src], es.at[j, src], er.at[j, src],
                device_id={"expert": src}, device_id_type=MESH).wait_recv()
            mixed += recvc[j, src].astype(F32) * weights[k + 1]
        out_ref[:, pl.ds(j * cw, cw)] = mixed.astype(BF16)

    for cp in pending:
        cp.wait_send()


def on_device(tokens, expert_ids, route_weights, w_gate, w_up, w_down):
    n_exp = lax.axis_size("expert")
    n_etp = lax.axis_size("etp")
    rows, width = tokens.shape
    own_rows = rows // n_etp
    exp_dev, ff, _ = w_gate.shape
    assert exp_dev == 1 and n_etp % 2 == 0
    n_x = n_etp // 2
    n_chunk = 4
    kq, cw, grp = width // n_etp, width // n_chunk, n_exp * own_rows
    half = n_x * grp
    dma = pltpu.SemaphoreType.DMA
    vmem = pl.BlockSpec(memory_space=pltpu.VMEM)
    hbm = pl.BlockSpec(memory_space=pl.ANY)
    return pl.pallas_call(
        functools.partial(layer_kernel, n_exp, n_etp, n_chunk),
        out_shape=pltpu.VMEM((own_rows, width), BF16),
        in_specs=[hbm] * 6,
        out_specs=vmem,
        scratch_shapes=[
            pltpu.VMEM((n_etp, n_exp, rows, kq), BF16),
            pltpu.VMEM((n_etp, ff, kq), BF16),
            pltpu.VMEM((n_etp, ff, kq), BF16),
            pltpu.VMEM((n_chunk, ff, cw), BF16),
            pltpu.VMEM((n_chunk, 2 * half, cw), BF16),
            pltpu.VMEM((n_chunk, half, cw), BF16),
            pltpu.VMEM((n_chunk, n_x - 1, grp, cw), BF16),
            pltpu.VMEM((n_chunk, n_x - 1, grp, cw), BF16),
            pltpu.VMEM((n_chunk, grp, cw), F32),
            pltpu.VMEM((n_chunk, n_exp, own_rows, cw), BF16),
            pltpu.VMEM((n_chunk, n_exp, own_rows, cw), BF16),
            pltpu.VMEM(expert_ids.shape[::-1], jnp.int32),
            pltpu.VMEM(route_weights.shape[::-1], F32),
            dma((2,)),
            dma((n_etp, 2)),
            dma((n_chunk,)),
            dma((n_etp,)),
            dma((n_exp,)), dma((n_exp,)),
            dma((n_x - 1, n_exp - 1)), dma((n_x - 1, n_exp - 1)),
            dma((n_x, n_exp - 1)), dma((n_x, n_exp - 1)),
            dma((n_chunk,)), dma((n_chunk,)),
            dma((n_chunk, n_x - 1)), dma((n_chunk, n_x - 1)),
            dma((n_chunk, n_exp)), dma((n_chunk, n_exp)),
        ],
        compiler_params=pltpu.CompilerParams(collective_id=0, has_side_effects=True),
    )(tokens, expert_ids.T, route_weights.T, w_gate, w_up, w_down)


def solution(mesh):
    in_specs = (
        P(("group", "expert"), None),
        P(("group", "expert"), None),
        P(("group", "expert", "etp"), None),
        P("expert", "etp", None),
        P("expert", "etp", None),
        P("expert", "etp", None),
    )
    out_specs = P(("group", "expert", "etp"), None)
    return jax.shard_map(
        on_device, mesh=mesh, in_specs=in_specs, out_specs=out_specs, check_vma=False
    )
```

```python
import functools

import jax
import jax.numpy as jnp
from jax import lax
from jax.experimental import pallas as pl
from jax.experimental.pallas import tpu as pltpu
from jax.sharding import PartitionSpec as P

MESH = pl.DeviceIdType.MESH
BF16 = jnp.bfloat16
F32 = jnp.float32


def layer_kernel(
    n_exp, n_etp, n_chunk,
    tok_ref, ids_ref, rw_ref, wg_ref, wu_ref, wd_ref, out_ref,
    xbuf, wb, wdb, pbuf, recva, sendb, recvb, ownb, sendc, recvc,
    acc, idsb, rwb, ssem, wsem, dsem, tsem, zs, zr, xs, xr, cs, cr, as_, ar, bs, br, es, er,
):
    n_x = n_etp // 2
    rows = tok_ref.shape[0]
    own_rows = rows // n_etp
    width = tok_ref.shape[1]
    kq = width // n_etp
    cw = width // n_chunk
    grp = n_exp * own_rows
    e = lax.axis_index("expert")
    q = lax.axis_index("etp")
    x = q // 2
    c = q % 2

    def etp_of(co, xo):
        return lax.rem(x + xo, n_x) * 2 + lax.rem(c + co, 2)

    high = e // (n_exp // 2)

    def farthest(k):
        down, up = n_exp - 1 - k, k
        down = down - (e - down + n_exp) // n_exp
        up = up + (up - e + n_exp) // n_exp
        return (1 - high) * down + high * up

    far = [farthest(k) for k in range(n_exp - 1)]
    near = far[::-1]

    def several(ref, sent, arrived):
        return pltpu.make_async_remote_copy(
            ref, ref, sent, arrived, device_id={"etp": etp_of(1, 0)}, device_id_type=MESH)

    slots = [(co, xo) for xo in range(n_x) for co in range(2)]

    def quarter(co, xo):
        return pl.ds(pl.multiple_of(etp_of(co, xo) * kq, kq), kq)

    tok_copies, d_copies = {}, []
    for co, xo in slots:
        i = co * n_x + xo
        t = pltpu.make_async_copy(tok_ref.at[:, quarter(co, xo)], xbuf.at[i, e], tsem.at[i])
        t.start()
        tok_copies[i] = t
    for co, xo in slots:
        i = co * n_x + xo
        for h, w_ref in enumerate((wg_ref, wu_ref)):
            pltpu.make_async_copy(w_ref.at[0, :, quarter(co, xo)], wb.at[i, h], wsem.at[i]).start()
    for j in range(n_chunk):
        d = pltpu.make_async_copy(wd_ref.at[0, :, pl.ds(j * cw, cw)], wdb.at[j], dsem.at[j])
        d.start()
        d_copies.append(d)

    small_copies = [pltpu.make_async_copy(ids_ref, idsb, ssem.at[0]),
                    pltpu.make_async_copy(rw_ref, rwb, ssem.at[1])]
    for cp in small_copies:
        cp.start()
    barrier = pltpu.get_barrier_semaphore()
    partners = [{"etp": etp_of(1, 0)}]
    partners += [{"etp": etp_of(0, xo)} for xo in range(1, n_x)]
    partners += [{"expert": lax.rem(e + k, n_exp)} for k in range(1, n_exp)]
    for dev in partners:
        pl.semaphore_signal(barrier, inc=1, device_id=dev, device_id_type=MESH)
    pl.semaphore_wait(barrier, len(partners))

    for to in far:
        cp = pltpu.make_async_remote_copy(
            tok_ref.at[:, quarter(0, 0)], xbuf.at[0, e], zs, zr.at[e],
            device_id={"expert": to}, device_id_type=MESH)
        cp.start()

    def z_arrival(src):
        return pltpu.make_async_remote_copy(
            tok_ref.at[:, quarter(0, 0)], xbuf.at[0, src], zs, zr.at[src],
            device_id={"expert": src}, device_id_type=MESH)

    x_copies = {}

    def to_core(xo, k):
        blk = near[k - 1]
        cp = pltpu.make_async_remote_copy(
            xbuf.at[xo, blk], xbuf.at[n_x + xo, blk], cs, cr.at[xo],
            device_id={"etp": etp_of(1, 0)}, device_id_type=MESH)
        cp.start()

    for k in range(1, n_exp):
        blk = near[k - 1]
        z_arrival(blk).wait_recv()
        for xo in range(1, n_x):
            cp = pltpu.make_async_remote_copy(
                xbuf.at[0, blk], xbuf.at[n_x - xo, blk], xs, xr.at[xo - 1, k - 1],
                device_id={"etp": etp_of(0, xo)}, device_id_type=MESH)
            cp.start()
            x_copies[xo, k] = cp
        to_core(0, k)

    def add_slot(co, xo):
        i = co * n_x + xo
        tok_copies[i].wait()
        pltpu.make_async_copy(wb.at[i], wb.at[i], wsem.at[i]).wait()
        xv = xbuf[i].reshape(n_exp * rows, kq)
        dims = (((1,), (1,)), ((), ()))
        for h in range(2):
            part = lax.dot_general(xv, wb[i, h], dims, preferred_element_type=F32)
            if i == 0:
                acc[h] = part
            else:
                acc[h] += part

    def from_core(xo):
        several(xbuf.at[n_x + xo, pl.ds(0, n_exp - 1)], cs, cr.at[xo]).wait_recv()

    add_slot(0, 0)
    from_core(0)
    add_slot(1, 0)
    for xo in range(1, n_x):
        for k in range(1, n_exp):
            x_copies[xo, k].wait_recv()
            to_core(n_x - xo, k)
    for xo in range(1, n_x):
        add_slot(0, xo)
    for xo in range(1, n_x):
        from_core(xo)
        add_slot(1, xo)
    gate, upper = acc[0], acc[1]
    hidden = (gate / (1.0 + jnp.exp(-gate)) * upper).astype(BF16)

    total = n_exp * rows
    m = lax.broadcasted_iota(jnp.int32, (total, total), 0)
    n = lax.broadcasted_iota(jnp.int32, (total, total), 1)
    slot = m // grp
    dest = lax.rem(x + slot % n_x, n_x) * 2 + lax.rem(c + slot // n_x, 2)
    source = (m % grp) // own_rows * rows + dest * own_rows + m % own_rows
    perm = (n == source).astype(F32).astype(BF16)
    hidden = jnp.dot(perm, hidden, preferred_element_type=F32).astype(BF16)

    half = n_x * grp
    a_copies, b_copies = [], {}
    for j in range(n_chunk):
        d_copies[j].wait()
        pbuf[j] = jnp.dot(hidden, wdb[j], preferred_element_type=F32).astype(BF16)
        cp = pltpu.make_async_remote_copy(
            pbuf.at[j, pl.ds(half, half)], recva.at[j], as_, ar.at[j],
            device_id={"etp": etp_of(1, 0)}, device_id_type=MESH)
        cp.start()
        a_copies.append(cp)

    for j in range(n_chunk):
        a_copies[j].wait_recv()
        for xo in range(1, n_x):
            at = pl.ds(xo * grp, grp)
            sendb[j, xo - 1] = (pbuf[j, at].astype(F32) + recva[j, at].astype(F32)).astype(BF16)
            cp = pltpu.make_async_remote_copy(
                sendb.at[j, xo - 1], recvb.at[j, xo - 1], bs, br.at[j, xo - 1],
                device_id={"etp": etp_of(0, xo)}, device_id_type=MESH)
            cp.start()
            b_copies[j, xo] = cp
        at = pl.ds(0, grp)
        ownb[j] = pbuf[j, at].astype(F32) + recva[j, at].astype(F32)

    for j in range(n_chunk):
        total_j = ownb[j]
        for xo in range(1, n_x):
            b_copies[j, xo].wait_recv()
            total_j += recvb[j, xo - 1].astype(F32)
        total_j = total_j.astype(BF16)
        for z in range(n_exp):
            sendc[j, z] = total_j[z * own_rows:(z + 1) * own_rows]
        for to in far:
            cp = pltpu.make_async_remote_copy(
                sendc.at[j, to], recvc.at[j, e], es, er.at[j],
                device_id={"expert": to}, device_id_type=MESH)
            cp.start()

    for cp in small_copies:
        cp.wait()
    top = idsb.shape[0]

    def column(row, first):
        lanes = lax.broadcasted_iota(jnp.int32, (own_rows, row.shape[1]), 1)
        here = lax.broadcasted_iota(jnp.int32, (own_rows, row.shape[1]), 0) + first
        return jnp.sum(jnp.where(lanes == here, row, jnp.zeros_like(row)), axis=1, keepdims=True)

    rws = rwb[...]
    combine = rws / jnp.sum(rws, axis=0, keepdims=True)
    chosen = [column(idsb[k:k + 1, :], q * own_rows) for k in range(top)]
    share = [column(combine[k:k + 1, :], 0) for k in range(top)]
    weights = []
    for src in [e] + near:
        weights.append(sum(jnp.where(i == src, w, 0.0) for i, w in zip(chosen, share)))

    for j in range(n_chunk):
        mixed = sendc[j, e].astype(F32) * weights[0]
        several(recvc.at[j, pl.ds(0, n_exp - 1)], es, er.at[j]).wait_recv()
        for k, src in enumerate(near):
            mixed += recvc[j, src].astype(F32) * weights[k + 1]
        out_ref[:, pl.ds(j * cw, cw)] = mixed.astype(BF16)

    remote = n_exp - 1
    several(xbuf.at[0, pl.ds(0, remote)], zs, zr.at[0]).wait_send()
    several(xbuf.at[pl.ds(0, n_x - 1), pl.ds(0, remote)], xs, xr.at[0, 0]).wait_send()
    several(xbuf.at[pl.ds(0, n_x), pl.ds(0, remote)], cs, cr.at[0]).wait_send()
    several(recva, as_, ar.at[0]).wait_send()
    several(sendb, bs, br.at[0, 0]).wait_send()
    several(sendc.at[:, pl.ds(0, remote)], es, er.at[0]).wait_send()


def on_device(tokens, expert_ids, route_weights, w_gate, w_up, w_down):
    n_exp = lax.axis_size("expert")
    n_etp = lax.axis_size("etp")
    rows, width = tokens.shape
    own_rows = rows // n_etp
    exp_dev, ff, _ = w_gate.shape
    assert exp_dev == 1 and n_etp % 2 == 0
    n_x = n_etp // 2
    n_chunk = 4
    kq, cw, grp = width // n_etp, width // n_chunk, n_exp * own_rows
    half = n_x * grp
    dma = pltpu.SemaphoreType.DMA
    vmem = pl.BlockSpec(memory_space=pltpu.VMEM)
    hbm = pl.BlockSpec(memory_space=pl.ANY)
    return pl.pallas_call(
        functools.partial(layer_kernel, n_exp, n_etp, n_chunk),
        out_shape=pltpu.VMEM((own_rows, width), BF16),
        in_specs=[hbm] * 6,
        out_specs=vmem,
        scratch_shapes=[
            pltpu.VMEM((n_etp, n_exp, rows, kq), BF16),
            pltpu.VMEM((n_etp, 2, ff, kq), BF16),
            pltpu.VMEM((n_chunk, ff, cw), BF16),
            pltpu.VMEM((n_chunk, 2 * half, cw), BF16),
            pltpu.VMEM((n_chunk, half, cw), BF16),
            pltpu.VMEM((n_chunk, n_x - 1, grp, cw), BF16),
            pltpu.VMEM((n_chunk, n_x - 1, grp, cw), BF16),
            pltpu.VMEM((n_chunk, grp, cw), F32),
            pltpu.VMEM((n_chunk, n_exp, own_rows, cw), BF16),
            pltpu.VMEM((n_chunk, n_exp, own_rows, cw), BF16),
            pltpu.VMEM((2, n_exp * rows, ff), F32),
            pltpu.VMEM(expert_ids.shape[::-1], jnp.int32),
            pltpu.VMEM(route_weights.shape[::-1], F32),
            dma((2,)),
            dma((n_etp,)),
            dma((n_chunk,)),
            dma((n_etp,)),
            dma, dma((n_exp,)),
            dma, dma((n_x - 1, n_exp - 1)),
            dma, dma((n_x,)),
            dma, dma((n_chunk,)),
            dma, dma((n_chunk, n_x - 1)),
            dma, dma((n_chunk,)),
        ],
        compiler_params=pltpu.CompilerParams(collective_id=0, has_side_effects=True),
    )(tokens, expert_ids.T, route_weights.T, w_gate, w_up, w_down)


def solution(mesh):
    in_specs = (
        P(("group", "expert"), None),
        P(("group", "expert"), None),
        P(("group", "expert", "etp"), None),
        P("expert", "etp", None),
        P("expert", "etp", None),
        P("expert", "etp", None),
    )
    out_specs = P(("group", "expert", "etp"), None)
    return jax.shard_map(
        on_device, mesh=mesh, in_specs=in_specs, out_specs=out_specs, check_vma=False
    )
```
